32 devices in a mesh: group: 2 (over x), slab: 16 (over z, y, core).
Axes of the slice: x: 2, y: 2, z: 4, core: 2. Of those that a mesh axis runs over, the one named last changes fastest.
Arguments:
- queries: bfloat16 [16384, 512], P(('group', 'slab')), may hold values from -6 to 6
- keys: bfloat16 [16384, 512], P(('group', 'slab')), may hold values from -6 to 6
- values: bfloat16 [16384, 512], P(('group', 'slab')), may hold values from -6 to 6
- neighbours: int32 [128, 6], P(('group', 'slab')), may hold values from 0 to 15, as said below
- live_tiles: int32 [32], P(('group', 'slab')), may hold values from 1 to 4, as said below
- boundary_ids: int32 [32, 4], P(('group', 'slab')), may hold values from 0 to 3, as said below
Outputs:
- attended: bfloat16 [16384, 512], P(('group', 'slab'))
The draws below stay inside these ranges and needn't reach their ends.
Inputs may be any that keep to these rules, and one draw needn't show every extreme that they name: `neighbours`: each row names 6 different positions of the pool. `live_tiles`: some slab has all 4 tiles active. `boundary_ids`: each row names 4 different tiles of its slab.
All inputs are finite; a program needn't handle non-finite values.
Results may differ from the reference program's by a relative error of at most 0.008.
Values may be sent and summed in bfloat16 or wider, within the bound.
A program may use at most 128 MiB of HBM per device.

```python
import jax
import jax.numpy as jnp
from jax import lax

HEADS = 8
HEAD_DIM = 64
TILE = 128
TILES_DEV = 4
HALO = 4
BOUNDARY = 4
LISTED = 6
BLOCK = 4
POOL = 16
NTILES = 128
NODES = 16384
N_GROUP = 2
N_SLAB = 16
DEVICES = 32


def draw_queries(key, part):
    width = HEADS * HEAD_DIM
    base = jax.random.normal(jax.random.fold_in(key, 11), (NODES, width), jnp.float32)
    return jnp.clip(base, -6.0, 6.0).astype(jnp.bfloat16)


def draw_keys(key, part):
    width = HEADS * HEAD_DIM
    base = jax.random.normal(jax.random.fold_in(key, 17), (NODES, width), jnp.float32)
    return jnp.clip(base, -6.0, 6.0).astype(jnp.bfloat16)


def draw_neighbours(key, part):
    row_keys = jax.random.split(jax.random.fold_in(key, 23), NTILES)
    picked = jax.vmap(lambda row_key: jax.random.permutation(row_key, POOL)[:LISTED])(row_keys)
    return picked.astype(jnp.int32)


def draw_live_tiles(key, part):
    counts = jax.random.randint(jax.random.fold_in(key, 29), (DEVICES,), 1, TILES_DEV + 1)
    fullest = jax.random.randint(jax.random.fold_in(key, 31), (), 0, DEVICES)
    return counts.at[fullest].set(TILES_DEV).astype(jnp.int32)


def draw_boundary_ids(key, part):
    row_keys = jax.random.split(jax.random.fold_in(key, 37), DEVICES)
    picked = jax.vmap(lambda row_key: jax.random.permutation(row_key, TILES_DEV)[:BOUNDARY])(row_keys)
    return picked.astype(jnp.int32)


def steps_of(rng, extent, cuts, low, high):
    loudness = 1.0
    for axis_at, shards_of in cuts:
        steps = jax.random.uniform(jax.random.fold_in(jax.random.fold_in(rng, 6), axis_at), (shards_of,), jnp.float32, low / len(cuts), high / len(cuts))
        loudness = loudness * jnp.repeat(jnp.exp(steps), extent[axis_at] // shards_of).reshape((-1,) + (1,) * (len(extent) - 1 - axis_at))
    return loudness


def bell_draw(own_key, shape, scale, bound, cuts=(), held_as=jnp.bfloat16):
    values = scale * jax.random.normal(own_key, shape, jnp.float32)
    if cuts:
        values = values * steps_of(own_key, shape, cuts, -0.22, 0.18)
    return jnp.clip(values, -bound, bound).astype(held_as)


def setup_inputs(seed: int = 0) -> dict:
    splits = jax.random.split(jax.random.key(seed), 7)
    return {
        "queries": draw_queries(jax.random.fold_in(splits[6], 71), 0),
        "keys": draw_keys(jax.random.fold_in(splits[6], 71), 0),
        "values": bell_draw(splits[2], (NODES, HEADS * HEAD_DIM), 1.0, 6.0, ((0, 32),)),
        "neighbours": draw_neighbours(jax.random.fold_in(splits[6], 71), 0),
        "live_tiles": draw_live_tiles(jax.random.fold_in(splits[6], 71), 0),
        "boundary_ids": draw_boundary_ids(jax.random.fold_in(splits[6], 71), 0),
    }


def attend(tile_queries, pool, lists, live):
    width = HEADS * HEAD_DIM

    def one_block(number):
        start = (number * BLOCK).astype(jnp.int32)
        query_block = lax.dynamic_slice_in_dim(tile_queries, start, BLOCK, 0)
        chosen = lax.dynamic_slice_in_dim(lists, start, BLOCK, 0)
        key_set = pool[0][chosen].reshape(BLOCK, LISTED * TILE, HEADS, HEAD_DIM)
        value_set = pool[1][chosen].reshape(BLOCK, LISTED * TILE, HEADS, HEAD_DIM)
        query_set = query_block.reshape(BLOCK, TILE, HEADS, HEAD_DIM)
        scores = jnp.einsum("qihd,qjhd->qhij", query_set.astype(jnp.float32), key_set.astype(jnp.float32)) * (HEAD_DIM ** -0.5)
        weights = jax.nn.softmax(scores, axis=-1).astype(jnp.bfloat16)
        mixed = jnp.einsum("qhij,qjhd->qihd", weights.astype(jnp.float32), value_set.astype(jnp.float32))
        alive = (start + jnp.arange(BLOCK, dtype=jnp.int32)) < live
        mixed = jnp.where(alive[:, None, None, None], mixed, 0.0)
        return mixed.astype(jnp.bfloat16).reshape(BLOCK, TILE, width)

    outputs = lax.map(one_block, jnp.arange(TILES_DEV // BLOCK, dtype=jnp.int32))
    return outputs.reshape(TILES_DEV * TILE, width)


def reference(queries, keys, values, neighbours, live_tiles, boundary_ids):
    width = HEADS * HEAD_DIM
    regions = N_GROUP
    slabs = N_SLAB
    pairs = jnp.stack([keys, values]).reshape(2, regions, slabs, TILES_DEV, TILE, width)
    query_tiles = queries.reshape(regions * slabs, TILES_DEV, TILE, width)
    lists = neighbours.reshape(regions * slabs, TILES_DEV, LISTED)
    borders = boundary_ids.reshape(regions, slabs, BOUNDARY)

    def one_slab(index):
        region = index // slabs
        within = index % slabs
        own_tiles = pairs[:, region, within]
        before = pairs[:, region, (within - 1) % slabs][:, TILES_DEV - HALO:]
        after = pairs[:, region, (within + 1) % slabs][:, :HALO]
        source = (region - 1) % regions
        remote = pairs[:, source, within]
        border = jnp.take(remote, borders[source, within], axis=1)
        pool = jnp.concatenate([own_tiles, before, after, border], axis=1)
        return attend(query_tiles[index], pool, lists[index], live_tiles[index])

    result = lax.map(one_slab, jnp.arange(regions * slabs, dtype=jnp.int32))
    return result.reshape(NODES, width)
```

```python
import functools
import math

import jax
import jax.numpy as jnp
from jax import lax
from jax.experimental import pallas as pl
from jax.experimental.pallas import tpu as pltpu
from jax.sharding import PartitionSpec as P

HEAD_DIM = 64
TILE = 128
NEVER = -1e38
LOWEST = -1e30
SCALE = HEAD_DIM ** (-0.5) * math.log2(math.e)
NT = (((1,), (1,)), ((), ()))
NN = (((1,), (0,)), ((), ()))


def dot(a, b, dims):
    return lax.dot_general(a, b, dims, preferred_element_type=jnp.float32)


def kernel(
    groups, slabs,
    q_ref, k_ref, v_ref, lists_ref, live_ref, ids_ref,
    out_ref,
    pool_k, pool_v, q_raw, q_pairs, acc, top, bias, far_ids,
    local_sem, send_sem, recv_sem, ids_sem,
):
    count = lists_ref.shape[0]
    listed = lists_ref.shape[1]
    pairs = q_pairs.shape[0]
    wide = 2 * HEAD_DIM
    group = lax.axis_index("group")
    slab = lax.axis_index("slab")
    odd = lax.rem(slab, 2)
    near = slab + 1 - 2 * odd
    far = lax.rem(slab - 1 + 2 * odd + slabs, slabs)
    ahead = lax.rem(group + 1, groups)
    behind = lax.rem(group - 1 + groups, groups)
    at_near = {"group": group, "slab": near}
    at_far = {"group": group, "slab": far}
    at_ahead = {"group": ahead, "slab": slab}
    at_behind = {"group": behind, "slab": slab}
    mesh_id = pl.DeviceIdType.MESH

    barrier = pltpu.get_barrier_semaphore()
    for device in (at_near, at_far, at_behind):
        pl.semaphore_signal(barrier, inc=1, device_id=device, device_id_type=mesh_id)

    def slot(place, number):
        if place < 2:
            return (place * count + number) // 2, lax.rem(place * count + number, 2)
        return count + number, place - 2

    def rows(place, number):
        chunk, half = slot(place, number)
        return chunk, pl.ds(half * TILE, TILE)

    def piece(ref, number):
        return ref.at[pl.ds(number * TILE, TILE)]

    def own(number, kind):
        ref, pool = ((k_ref, pool_k), (v_ref, pool_v))[kind]
        chunk, at = rows(0, number)
        return pltpu.make_async_copy(piece(ref, number), pool.at[chunk, at], local_sem.at[kind, number])

    def remote(place, number, kind):
        ref, pool = ((k_ref, pool_k), (v_ref, pool_v))[kind]
        chunk, at = rows(place, number)
        return pltpu.make_async_remote_copy(
            src_ref=piece(ref, number),
            dst_ref=pool.at[chunk, at],
            send_sem=send_sem.at[place - 1, kind, number],
            recv_sem=recv_sem.at[place - 1, kind, number],
            device_id=(at_near, at_far, at_ahead)[place - 1],
            device_id_type=mesh_id,
        )

    q_copy = pltpu.make_async_copy(q_ref, q_raw, local_sem.at[2, 0])
    q_copy.start()
    for number in range(count):
        for kind in range(2):
            own(number, kind).start()

    ids_copy = pltpu.make_async_remote_copy(
        src_ref=ids_ref, dst_ref=far_ids, send_sem=ids_sem.at[0], recv_sem=ids_sem.at[1],
        device_id=at_ahead, device_id_type=mesh_id,
    )
    pl.semaphore_wait(barrier, 3)
    ids_copy.start()
    for number in range(count):
        for place in (3, 2, 1):
            for kind in range(2):
                remote(place, number, kind).start()

    def listing(tile, position):
        hit = lists_ref[tile, 0] == position
        for entry in range(1, listed):
            hit = jnp.logical_or(hit, lists_ref[tile, entry] == position)
        return jnp.where(hit, 0.0, NEVER).astype(jnp.float32)

    near_at = 2 * count - odd * count
    far_at = count + odd * count
    for tile in range(count):
        for number in range(count):
            for place, first in ((0, 0), (1, near_at), (2, far_at)):
                chunk, half = slot(place, number)
                bias[tile, chunk, pl.ds(half, 1)] = jnp.full((1, 2 * TILE), listing(tile, first + number))

    q_copy.wait()
    low = lax.broadcasted_iota(jnp.int32, (TILE, wide), 1) < HEAD_DIM
    for pair in range(pairs):
        for tile in range(count):
            block = q_raw[pl.ds(tile * TILE, TILE), pl.ds(pair * wide, wide)]
            zero = jnp.zeros_like(block)
            q_pairs[pair, tile, pl.ds(0, TILE)] = jnp.where(low, block, zero)
            q_pairs[pair, tile, pl.ds(TILE, TILE)] = jnp.where(low, zero, block)
    acc[...] = jnp.zeros_like(acc)
    top[...] = jnp.full(top.shape, LOWEST, jnp.float32)

    ones = jnp.ones((16, 2 * TILE), jnp.bfloat16)

    def update(chunk, pair, tile, values):
        keys = pool_k[chunk, :, pl.ds(pl.multiple_of(pair * wide, wide), wide)]
        scores = dot(keys, q_pairs[pair, tile], NT)
        first, second = scores[:TILE], scores[TILE:]
        first_bias, second_bias = bias[tile, chunk, 0:1], bias[tile, chunk, 1:2]
        before = top[pair, tile, 0:1]
        after = jnp.maximum(
            before,
            jnp.maximum(
                jnp.max(first, axis=0, keepdims=True) + first_bias,
                jnp.max(second, axis=0, keepdims=True) + second_bias,
            ),
        )
        shrink = jnp.exp2((before - after) * SCALE)
        weights = jnp.concatenate(
            [
                jnp.exp2((first - (after - first_bias)) * SCALE).astype(jnp.bfloat16),
                jnp.exp2((second - (after - second_bias)) * SCALE).astype(jnp.bfloat16),
            ],
            axis=0,
        )
        mixed = dot(values, weights, NN)
        upper = acc[pair, tile, :HEAD_DIM] * shrink + jnp.concatenate(
            [mixed[:HEAD_DIM, :TILE], mixed[HEAD_DIM:wide, TILE:]], axis=1
        )
        total = acc[pair, tile, HEAD_DIM:] * shrink + mixed[wide:wide + 8]
        return after, upper, total

    def chunk_values(chunk, pair):
        block = pool_v[chunk, :, pl.ds(pl.multiple_of(pair * wide, wide), wide)]
        return jnp.concatenate([block.T, ones], axis=0)

    def run(chunk):
        def one_pair(pair, carry):
            values = chunk_values(chunk, pair)
            for tile in range(count):
                after, upper, total = update(chunk, pair, tile, values)
                top[pair, tile, 0:1] = after
                acc[pair, tile, :HEAD_DIM] = upper
                acc[pair, tile, HEAD_DIM:] = total
            return carry

        lax.fori_loop(0, pairs, one_pair, 0)

    for number in range(count):
        for kind in range(2):
            own(number, kind).wait()
    lax.fori_loop(0, count // 2, lambda i, c: (run(i), c)[1], 0)
    for number in range(count):
        for kind in range(2):
            remote(1, number, kind).wait()
    lax.fori_loop(count // 2, count, lambda i, c: (run(i), c)[1], 0)

    ids_copy.wait()
    for tile in range(count):
        given = [listing(tile, 3 * count + entry) for entry in range(count)]
        for number in range(count):
            row = jnp.full((1, 2 * TILE), NEVER, jnp.float32)
            for entry in range(count):
                hit = jnp.broadcast_to(far_ids[0:1, entry:entry + 1], (1, 2 * TILE)) == number
                row = jnp.where(hit, given[entry], row)
            bias[tile, count + number, 1:2] = row

    def later(number, carry):
        for place in (2, 3):
            for kind in range(2):
                remote(place, number, kind).wait()
        run(count + number)
        return carry

    lax.fori_loop(0, count - 1, later, 0)
    for place in (2, 3):
        for kind in range(2):
            remote(place, count - 1, kind).wait()

    live = live_ref[0]

    def last(pair, carry):
        chunk = 2 * count - 1
        values = chunk_values(chunk, pair)
        for tile in range(count):
            _, upper, total = update(chunk, pair, tile, values)
            mixed = upper / total[0:1]
            mixed = jnp.concatenate([mixed[:, :TILE], mixed[:, TILE:]], axis=0)
            mixed = jnp.where(tile < live, mixed.T, 0.0)
            at = pl.ds(pl.multiple_of(pair * wide, wide), wide)
            out_ref[pl.ds(tile * TILE, TILE), at] = mixed.astype(out_ref.dtype)
        return carry

    lax.fori_loop(0, pairs, last, 0)


def solution(mesh):
    groups, slabs = mesh.shape["group"], mesh.shape["slab"]

    def shards(queries, keys, values, neighbours, live_tiles, boundary_ids):
        nodes, width = queries.shape
        count = neighbours.shape[0]
        pairs = width // (2 * HEAD_DIM)
        anywhere = pl.BlockSpec(memory_space=pl.ANY)
        scalars = pl.BlockSpec(memory_space=pltpu.SMEM)
        inside = pl.BlockSpec(memory_space=pltpu.VMEM)
        return pl.pallas_call(
            functools.partial(kernel, groups, slabs),
            out_shape=jax.ShapeDtypeStruct((nodes, width), queries.dtype),
            in_specs=[anywhere, anywhere, anywhere, scalars, scalars, inside],
            out_specs=inside,
            scratch_shapes=[
                pltpu.VMEM((2 * count, 2 * TILE, width), keys.dtype),
                pltpu.VMEM((2 * count, 2 * TILE, width), values.dtype),
                pltpu.VMEM((nodes, width), queries.dtype),
                pltpu.VMEM((pairs, count, 2 * TILE, 2 * HEAD_DIM), queries.dtype),
                pltpu.VMEM((pairs, count, HEAD_DIM + 8, 2 * TILE), jnp.float32),
                pltpu.VMEM((pairs, count, 8, 2 * TILE), jnp.float32),
                pltpu.VMEM((count, 2 * count, 2, 2 * TILE), jnp.float32),
                pltpu.VMEM(boundary_ids.shape, jnp.int32),
                pltpu.SemaphoreType.DMA((3, count)),
                pltpu.SemaphoreType.DMA((3, 2, count)),
                pltpu.SemaphoreType.DMA((3, 2, count)),
                pltpu.SemaphoreType.DMA((2,)),
            ],
            compiler_params=pltpu.CompilerParams(collective_id=0, has_side_effects=True),
        )(queries, keys, values, neighbours, live_tiles, boundary_ids)

    rows = P(("group", "slab"), None)
    return jax.shard_map(
        shards,
        mesh=mesh,
        in_specs=(rows, rows, rows, rows, P(("group", "slab")), rows),
        out_specs=rows,
        check_vma=False,
    )
```

```python
import functools
import math

import jax
import jax.numpy as jnp
from jax import lax
from jax.experimental import pallas as pl
from jax.experimental.pallas import tpu as pltpu
from jax.sharding import PartitionSpec as P

HEAD_DIM = 64
TILE = 128
NEVER = -1e38
LOWEST = -1e30
SCALE = HEAD_DIM ** (-0.5) * math.log2(math.e)
NT = (((1,), (1,)), ((), ()))
NN = (((1,), (0,)), ((), ()))


def dot(a, b, dims):
    return lax.dot_general(a, b, dims, preferred_element_type=jnp.float32)


def kernel(
    groups, slabs,
    q_ref, k_ref, v_ref, lists_ref, live_ref, ids_ref,
    out_ref,
    pool_k, pool_v, q_raw, q_pairs, acc, top, bias, far_ids,
    local_sem, send_sem, recv_sem, ids_sem,
):
    count = lists_ref.shape[0]
    listed = lists_ref.shape[1]
    pairs = q_pairs.shape[0]
    wide = 2 * HEAD_DIM
    group = lax.axis_index("group")
    slab = lax.axis_index("slab")
    odd = lax.rem(slab, 2)
    near = slab + 1 - 2 * odd
    far = lax.rem(slab - 1 + 2 * odd + slabs, slabs)
    ahead = lax.rem(group + 1, groups)
    behind = lax.rem(group - 1 + groups, groups)
    at_near = {"group": group, "slab": near}
    at_far = {"group": group, "slab": far}
    at_ahead = {"group": ahead, "slab": slab}
    at_behind = {"group": behind, "slab": slab}
    mesh_id = pl.DeviceIdType.MESH

    barrier = pltpu.get_barrier_semaphore()
    for device in (at_near, at_far, at_behind):
        pl.semaphore_signal(barrier, inc=1, device_id=device, device_id_type=mesh_id)

    def slot(place, number):
        if place < 2:
            return (place * count + number) // 2, (place * count + number) % 2
        return count + number, place - 2

    def rows(place, number):
        chunk, half = slot(place, number)
        return chunk, pl.ds(half * TILE, TILE)

    def piece(ref, number):
        return ref.at[pl.ds(number * TILE, TILE)]

    def own(number, kind):
        ref, pool = ((k_ref, pool_k), (v_ref, pool_v))[kind]
        chunk, at = rows(0, number)
        return pltpu.make_async_copy(piece(ref, number), pool.at[chunk, at], local_sem.at[kind, number])

    def remote(place, number, kind):
        ref, pool = ((k_ref, pool_k), (v_ref, pool_v))[kind]
        chunk, at = rows(place, number)
        return pltpu.make_async_remote_copy(
            src_ref=piece(ref, number),
            dst_ref=pool.at[chunk, at],
            send_sem=send_sem.at[place - 1, kind, number],
            recv_sem=recv_sem.at[place - 1, kind, number],
            device_id=(at_near, at_far, at_ahead)[place - 1],
            device_id_type=mesh_id,
        )

    q_copy = pltpu.make_async_copy(q_ref, q_raw, local_sem.at[2, 0])
    q_copy.start()
    for number in range(count):
        for kind in range(2):
            own(number, kind).start()

    ids_copy = pltpu.make_async_remote_copy(
        src_ref=ids_ref, dst_ref=far_ids, send_sem=ids_sem.at[0], recv_sem=ids_sem.at[1],
        device_id=at_ahead, device_id_type=mesh_id,
    )
    pl.semaphore_wait(barrier, 3)
    ids_copy.start()
    for number in range(count):
        for place in (3, 2, 1):
            for kind in range(2):
                remote(place, number, kind).start()

    def listing(tile, position):
        hit = lists_ref[tile, 0] == position
        for entry in range(1, listed):
            hit = jnp.logical_or(hit, lists_ref[tile, entry] == position)
        return jnp.where(hit, 0.0, NEVER).astype(jnp.float32)

    near_at = 2 * count - odd * count
    far_at = count + odd * count
    for tile in range(count):
        for number in range(count):
            for place, first in ((0, 0), (1, near_at), (2, far_at)):
                chunk, half = slot(place, number)
                bias[tile, chunk, :, half * TILE:(half + 1) * TILE] = jnp.full((8, TILE), listing(tile, first + number))

    q_copy.wait()
    low = lax.broadcasted_iota(jnp.int32, (TILE, wide), 1) < HEAD_DIM
    for pair in range(pairs):
        for tile in range(count):
            block = q_raw[pl.ds(tile * TILE, TILE), pl.ds(pair * wide, wide)]
            zero = jnp.zeros_like(block)
            q_pairs[pair, tile, pl.ds(0, TILE)] = jnp.where(low, block, zero)
            q_pairs[pair, tile, pl.ds(TILE, TILE)] = jnp.where(low, zero, block)
    acc[...] = jnp.zeros_like(acc)
    top[...] = jnp.full(top.shape, LOWEST, jnp.float32)

    def operands(chunk, pair):
        at = pl.ds(pl.multiple_of(pair * wide, wide), wide)
        block = pool_v[chunk, :, at]
        left = lax.broadcasted_iota(jnp.int32, block.shape, 1) < HEAD_DIM
        one = jnp.ones_like(block)
        return pool_k[chunk, :, at], (jnp.where(left, block, one), jnp.where(left, one, block))

    def update(chunk, pair, tile, keys, values):
        scores = dot(q_pairs[pair, tile], keys, NT) + bias[tile, chunk, 0:1]
        peak = jnp.max(scores, axis=1, keepdims=True)
        before = top[pair, tile]
        after = jnp.maximum(before, peak)
        shrink = jnp.exp2((before - after) * SCALE)
        weights = jnp.concatenate(
            [
                jnp.exp2((scores[:, :TILE] - after) * SCALE).astype(jnp.bfloat16),
                jnp.exp2((scores[:, TILE:] - after) * SCALE).astype(jnp.bfloat16),
            ],
            axis=1,
        )
        upper = acc[pair, tile, :TILE] * shrink[:TILE] + dot(weights[:TILE], values[0], NN)
        lower = acc[pair, tile, TILE:] * shrink[TILE:] + dot(weights[TILE:], values[1], NN)
        return after, upper, lower

    def run(chunk):
        def one_pair(pair, carry):
            keys, values = operands(chunk, pair)
            for tile in range(count):
                after, upper, lower = update(chunk, pair, tile, keys, values)
                top[pair, tile] = after
                acc[pair, tile, :TILE] = upper
                acc[pair, tile, TILE:] = lower
            return carry

        lax.fori_loop(0, pairs, one_pair, 0)

    for number in range(count):
        for kind in range(2):
            own(number, kind).wait()
    lax.fori_loop(0, count // 2, lambda i, c: (run(i), c)[1], 0)
    for number in range(count):
        for kind in range(2):
            remote(1, number, kind).wait()
    lax.fori_loop(count // 2, count, lambda i, c: (run(i), c)[1], 0)

    ids_copy.wait()
    for tile in range(count):
        given = [listing(tile, 3 * count + entry) for entry in range(count)]
        for number in range(count):
            row = jnp.full((1, TILE), NEVER, jnp.float32)
            for entry in range(count):
                hit = jnp.broadcast_to(far_ids[0:1, entry:entry + 1], (1, TILE)) == number
                row = jnp.where(hit, given[entry], row)
            bias[tile, count + number, 0:1, TILE:] = row

    def later(number, carry):
        for place in (2, 3):
            for kind in range(2):
                remote(place, number, kind).wait()
        run(count + number)
        return carry

    lax.fori_loop(0, count - 1, later, 0)
    for place in (2, 3):
        for kind in range(2):
            remote(place, count - 1, kind).wait()

    live = live_ref[0]

    def last(pair, carry):
        chunk = 2 * count - 1
        keys, values = operands(chunk, pair)
        for tile in range(count):
            _, upper, lower = update(chunk, pair, tile, keys, values)
            mixed = jnp.where(low, upper, lower)
            total = pltpu.roll(jnp.where(low, lower, upper), HEAD_DIM, axis=1)
            mixed = jnp.where(tile < live, mixed / total, 0.0)
            at = pl.ds(pl.multiple_of(pair * wide, wide), wide)
            out_ref[pl.ds(tile * TILE, TILE), at] = mixed.astype(out_ref.dtype)
        return carry

    lax.fori_loop(0, pairs, last, 0)


def solution(mesh):
    groups, slabs = mesh.shape["group"], mesh.shape["slab"]

    def shards(queries, keys, values, neighbours, live_tiles, boundary_ids):
        nodes, width = queries.shape
        count = neighbours.shape[0]
        pairs = width // (2 * HEAD_DIM)
        anywhere = pl.BlockSpec(memory_space=pl.ANY)
        scalars = pl.BlockSpec(memory_space=pltpu.SMEM)
        inside = pl.BlockSpec(memory_space=pltpu.VMEM)
        return pl.pallas_call(
            functools.partial(kernel, groups, slabs),
            out_shape=jax.ShapeDtypeStruct((nodes, width), queries.dtype),
            in_specs=[anywhere, anywhere, anywhere, scalars, scalars, inside],
            out_specs=inside,
            scratch_shapes=[
                pltpu.VMEM((2 * count, 2 * TILE, width), keys.dtype),
                pltpu.VMEM((2 * count, 2 * TILE, width), values.dtype),
                pltpu.VMEM((nodes, width), queries.dtype),
                pltpu.VMEM((pairs, count, 2 * TILE, 2 * HEAD_DIM), queries.dtype),
                pltpu.VMEM((pairs, count, 2 * TILE, 2 * HEAD_DIM), jnp.float32),
                pltpu.VMEM((pairs, count, 2 * TILE, TILE), jnp.float32),
                pltpu.VMEM((count, 2 * count, 8, 2 * TILE), jnp.float32),
                pltpu.VMEM(boundary_ids.shape, jnp.int32),
                pltpu.SemaphoreType.DMA((3, count)),
                pltpu.SemaphoreType.DMA((3, 2, count)),
                pltpu.SemaphoreType.DMA((3, 2, count)),
                pltpu.SemaphoreType.DMA((2,)),
            ],
            compiler_params=pltpu.CompilerParams(collective_id=0, has_side_effects=True),
        )(queries, keys, values, neighbours, live_tiles, boundary_ids)

    rows = P(("group", "slab"), None)
    return jax.shard_map(
        shards,
        mesh=mesh,
        in_specs=(rows, rows, rows, rows, P(("group", "slab")), rows),
        out_specs=rows,
        check_vma=False,
    )
```

```python
import functools
import math

import jax
import jax.numpy as jnp
from jax import lax
from jax.experimental import pallas as pl
from jax.experimental.pallas import tpu as pltpu
from jax.sharding import PartitionSpec as P

HEAD_DIM = 64
TILE = 128
SCALE = HEAD_DIM ** (-0.5) * math.log2(math.e)
NT = (((1,), (1,)), ((), ()))
NN = (((1,), (0,)), ((), ()))


def dot(a, b, dims):
    return lax.dot_general(a, b, dims, preferred_element_type=jnp.float32)


def kernel(
    groups, slabs,
    q_ref, k_ref, v_ref, lists_ref, live_ref, ids_ref,
    out_ref,
    pool_k, pool_v, q_raw, q_pairs, weights, far_ids, near_ids,
    local_sem, send_sem, recv_sem, ids_sem,
):
    count = lists_ref.shape[0]
    listed = lists_ref.shape[1]
    pairs = q_pairs.shape[0]
    wide = 2 * HEAD_DIM
    group = lax.axis_index("group")
    slab = lax.axis_index("slab")
    odd = lax.rem(slab, 2)
    near = slab + 1 - 2 * odd
    far = lax.rem(slab - 1 + 2 * odd + slabs, slabs)
    ahead = lax.rem(group + 1, groups)
    behind = lax.rem(group - 1 + groups, groups)
    at_near = {"group": group, "slab": near}
    at_far = {"group": group, "slab": far}
    at_ahead = {"group": ahead, "slab": slab}
    at_behind = {"group": behind, "slab": slab}
    mesh_id = pl.DeviceIdType.MESH

    barrier = pltpu.get_barrier_semaphore()
    for device in (at_near, at_far, at_behind):
        pl.semaphore_signal(barrier, inc=1, device_id=device, device_id_type=mesh_id)

    sources = ((k_ref, pool_k), (v_ref, pool_v))

    def own(kind):
        ref, pool = sources[kind]
        return pltpu.make_async_copy(ref, pool.at[pl.ds(0, count)], local_sem.at[kind])

    def remote(place, kind):
        ref, pool = sources[kind]
        return pltpu.make_async_remote_copy(
            src_ref=ref,
            dst_ref=pool.at[pl.ds(place * count, count)],
            send_sem=send_sem.at[place - 1, kind],
            recv_sem=recv_sem.at[place - 1, kind],
            device_id=(at_near, at_far, at_ahead)[place - 1],
            device_id_type=mesh_id,
        )

    q_copy = pltpu.make_async_copy(q_ref, q_raw, local_sem.at[2])
    q_copy.start()
    own(0).start()
    own(1).start()
    ids_copy = pltpu.make_async_remote_copy(
        src_ref=ids_ref, dst_ref=far_ids, send_sem=ids_sem.at[0], recv_sem=ids_sem.at[1],
        device_id=at_ahead, device_id_type=mesh_id,
    )
    pl.semaphore_wait(barrier, 3)
    ids_copy.start()
    for kind in range(2):
        for place in (3, 2, 1):
            remote(place, kind).start()

    q_copy.wait()
    low = lax.broadcasted_iota(jnp.int32, (TILE, wide), 1) < HEAD_DIM
    for pair in range(pairs):
        for tile in range(count):
            block = q_raw[pl.ds(tile * TILE, TILE), pl.ds(pair * wide, wide)]
            zero = jnp.zeros_like(block)
            q_pairs[pair, tile, pl.ds(0, TILE)] = jnp.where(low, block, zero)
            q_pairs[pair, tile, pl.ds(TILE, TILE)] = jnp.where(low, zero, block)

    ids_copy.wait()
    ids_local = pltpu.make_async_copy(far_ids, near_ids, local_sem.at[3])
    ids_local.start()
    ids_local.wait()
    swap = count * (1 - odd)

    def slot(tile, entry):
        place = lists_ref[tile, entry]
        found = jnp.where(place < 2 * count, place + swap, place - swap)
        found = jnp.where(place < count, place, found)
        for number in range(count):
            found = jnp.where(place == 3 * count + number, 3 * count + near_ids[0, number], found)
        return found

    def gathered(pool, tile, at):
        return jnp.concatenate([pool[slot(tile, entry), :, at] for entry in range(listed)], axis=0)

    live = live_ref[0]

    def weigh(pair, carry):
        at = pl.ds(pl.multiple_of(pair * wide, wide), wide)
        for tile in range(count):
            scores = dot(q_pairs[pair, tile], gathered(pool_k, tile, at), NT)
            peak = jnp.max(scores, axis=1, keepdims=True)
            raised = jnp.exp2((scores - peak) * SCALE)
            total = jnp.sum(raised, axis=1, keepdims=True)
            share = jnp.where(tile < live, 1.0 / total, 0.0)
            weights[pair, tile] = (raised * share).astype(jnp.bfloat16)
        return carry

    def mix(pair, carry):
        at = pl.ds(pl.multiple_of(pair * wide, wide), wide)
        for tile in range(count):
            mixed = dot(weights[pair, tile], gathered(pool_v, tile, at), NN)
            mixed = jnp.where(low, mixed[:TILE], mixed[TILE:])
            out_ref[pl.ds(tile * TILE, TILE), at] = mixed.astype(out_ref.dtype)
        return carry

    for kind, step in ((0, weigh), (1, mix)):
        own(kind).wait()
        for place in (1, 2, 3):
            remote(place, kind).wait()
        lax.fori_loop(0, pairs, step, 0)


def solution(mesh):
    groups, slabs = mesh.shape["group"], mesh.shape["slab"]

    def shards(queries, keys, values, neighbours, live_tiles, boundary_ids):
        nodes, width = queries.shape
        count = neighbours.shape[0]
        pairs = width // (2 * HEAD_DIM)
        anywhere = pl.BlockSpec(memory_space=pl.ANY)
        scalars = pl.BlockSpec(memory_space=pltpu.SMEM)
        inside = pl.BlockSpec(memory_space=pltpu.VMEM)
        return pl.pallas_call(
            functools.partial(kernel, groups, slabs),
            out_shape=jax.ShapeDtypeStruct((nodes, width), queries.dtype),
            in_specs=[anywhere, anywhere, anywhere, scalars, scalars, inside],
            out_specs=inside,
            scratch_shapes=[
                pltpu.VMEM((4 * count, TILE, width), keys.dtype),
                pltpu.VMEM((4 * count, TILE, width), values.dtype),
                pltpu.VMEM((nodes, width), queries.dtype),
                pltpu.VMEM((pairs, count, 2 * TILE, 2 * HEAD_DIM), queries.dtype),
                pltpu.VMEM((pairs, count, 2 * TILE, neighbours.shape[1] * TILE), jnp.bfloat16),
                pltpu.VMEM(boundary_ids.shape, jnp.int32),
                pltpu.SMEM(boundary_ids.shape, jnp.int32),
                pltpu.SemaphoreType.DMA((4,)),
                pltpu.SemaphoreType.DMA((3, 2)),
                pltpu.SemaphoreType.DMA((3, 2)),
                pltpu.SemaphoreType.DMA((2,)),
            ],
            compiler_params=pltpu.CompilerParams(collective_id=0, has_side_effects=True),
        )(queries, keys.reshape(count, TILE, width), values.reshape(count, TILE, width), neighbours, live_tiles, boundary_ids)

    rows = P(("group", "slab"), None)
    return jax.shard_map(
        shards,
        mesh=mesh,
        in_specs=(rows, rows, rows, rows, P(("group", "slab")), rows),
        out_specs=rows,
        check_vma=False,
    )
```

```python
import functools
import math

import jax
import jax.numpy as jnp
from jax import lax
from jax.experimental import pallas as pl
from jax.experimental.pallas import tpu as pltpu
from jax.sharding import PartitionSpec as P

HEAD_DIM = 64
TILE = 128
SCALE = HEAD_DIM ** (-0.5) * math.log2(math.e)
NT = (((1,), (1,)), ((), ()))
NN = (((1,), (0,)), ((), ()))


def dot(a, b, dims):
    return lax.dot_general(a, b, dims, preferred_element_type=jnp.float32)


def kernel(
    groups, slabs,
    q_ref, k_ref, v_ref, lists_ref, live_ref, ids_ref,
    out_ref,
    pool_k, pool_v, q_raw, q_pairs, weights, far_ids, near_ids,
    local_sem, send_sem, recv_sem, ids_sem,
):
    count = lists_ref.shape[0]
    listed = lists_ref.shape[1]
    pairs = q_pairs.shape[0]
    wide = 2 * HEAD_DIM
    group = lax.axis_index("group")
    slab = lax.axis_index("slab")
    odd = lax.rem(slab, 2)
    near = slab + 1 - 2 * odd
    far = lax.rem(slab - 1 + 2 * odd + slabs, slabs)
    ahead = lax.rem(group + 1, groups)
    behind = lax.rem(group - 1 + groups, groups)
    at_near = {"group": group, "slab": near}
    at_far = {"group": group, "slab": far}
    at_ahead = {"group": ahead, "slab": slab}
    at_behind = {"group": behind, "slab": slab}
    mesh_id = pl.DeviceIdType.MESH

    barrier = pltpu.get_barrier_semaphore()
    for device in (at_near, at_far, at_behind):
        pl.semaphore_signal(barrier, inc=1, device_id=device, device_id_type=mesh_id)

    sources = ((k_ref, pool_k), (v_ref, pool_v))

    def own(kind):
        ref, pool = sources[kind]
        return pltpu.make_async_copy(ref, pool.at[pl.ds(0, count)], local_sem.at[kind])

    def remote(place, kind):
        ref, pool = sources[kind]
        return pltpu.make_async_remote_copy(
            src_ref=ref,
            dst_ref=pool.at[pl.ds(place * count, count)],
            send_sem=send_sem.at[place - 1, kind],
            recv_sem=recv_sem.at[place - 1, kind],
            device_id=(at_near, at_far, at_ahead)[place - 1],
            device_id_type=mesh_id,
        )

    q_copy = pltpu.make_async_copy(q_ref, q_raw, local_sem.at[2])
    q_copy.start()
    own(0).start()
    own(1).start()
    ids_copy = pltpu.make_async_remote_copy(
        src_ref=ids_ref, dst_ref=far_ids, send_sem=ids_sem.at[0], recv_sem=ids_sem.at[1],
        device_id=at_ahead, device_id_type=mesh_id,
    )
    pl.semaphore_wait(barrier, 3)
    ids_copy.start()
    for kind in range(2):
        for place in (3, 2, 1):
            remote(place, kind).start()

    q_copy.wait()
    low = lax.broadcasted_iota(jnp.int32, (TILE, wide), 1) < HEAD_DIM
    for pair in range(pairs):
        for tile in range(count):
            block = q_raw[pl.ds(tile * TILE, TILE), pl.ds(pair * wide, wide)]
            zero = jnp.zeros_like(block)
            q_pairs[pair, tile, pl.ds(0, TILE)] = jnp.where(low, block, zero)
            q_pairs[pair, tile, pl.ds(TILE, TILE)] = jnp.where(low, zero, block)

    ids_copy.wait()
    ids_local = pltpu.make_async_copy(far_ids, near_ids, local_sem.at[3])
    ids_local.start()
    ids_local.wait()
    swap = count * (1 - odd)

    def slot(tile, entry):
        place = lists_ref[tile, entry]
        found = jnp.where(place < 2 * count, place + swap, place - swap)
        found = jnp.where(place < count, place, found)
        for number in range(count):
            found = jnp.where(place == 3 * count + number, 3 * count + near_ids[0, number], found)
        return found

    def gathered(pool, tile, at):
        return jnp.concatenate([pool[slot(tile, entry), :, at] for entry in range(listed)], axis=0)

    live = live_ref[0]

    def weigh(pair, carry):
        at = pl.ds(pair * wide, wide)
        for tile in range(count):
            scores = dot(q_pairs[pair, tile], gathered(pool_k, tile, at), NT)
            peak = jnp.max(scores, axis=1, keepdims=True)
            raised = jnp.exp2((scores - peak) * SCALE)
            total = jnp.sum(raised, axis=1, keepdims=True)
            share = jnp.where(tile < live, 1.0 / total, 0.0)
            weights[pair, tile] = (raised * share).astype(jnp.bfloat16)
        return carry

    def mix(pair, carry):
        at = pl.ds(pair * wide, wide)
        for tile in range(count):
            mixed = dot(weights[pair, tile], gathered(pool_v, tile, at), NN)
            mixed = jnp.where(low, mixed[:TILE], mixed[TILE:])
            out_ref[pl.ds(tile * TILE, TILE), at] = mixed.astype(out_ref.dtype)
        return carry

    for kind, step in ((0, weigh), (1, mix)):
        own(kind).wait()
        for place in (1, 2, 3):
            remote(place, kind).wait()
        for pair in range(pairs):
            step(pair, 0)


def solution(mesh):
    groups, slabs = mesh.shape["group"], mesh.shape["slab"]

    def shards(queries, keys, values, neighbours, live_tiles, boundary_ids):
        nodes, width = queries.shape
        count = neighbours.shape[0]
        pairs = width // (2 * HEAD_DIM)
        anywhere = pl.BlockSpec(memory_space=pl.ANY)
        scalars = pl.BlockSpec(memory_space=pltpu.SMEM)
        inside = pl.BlockSpec(memory_space=pltpu.VMEM)
        return pl.pallas_call(
            functools.partial(kernel, groups, slabs),
            out_shape=jax.ShapeDtypeStruct((nodes, width), queries.dtype),
            in_specs=[anywhere, anywhere, anywhere, scalars, scalars, inside],
            out_specs=inside,
            scratch_shapes=[
                pltpu.VMEM((4 * count, TILE, width), keys.dtype),
                pltpu.VMEM((4 * count, TILE, width), values.dtype),
                pltpu.VMEM((nodes, width), queries.dtype),
                pltpu.VMEM((pairs, count, 2 * TILE, 2 * HEAD_DIM), queries.dtype),
                pltpu.VMEM((pairs, count, 2 * TILE, neighbours.shape[1] * TILE), jnp.bfloat16),
                pltpu.VMEM(boundary_ids.shape, jnp.int32),
                pltpu.SMEM(boundary_ids.shape, jnp.int32),
                pltpu.SemaphoreType.DMA((4,)),
                pltpu.SemaphoreType.DMA((3, 2)),
                pltpu.SemaphoreType.DMA((3, 2)),
                pltpu.SemaphoreType.DMA((2,)),
            ],
            compiler_params=pltpu.CompilerParams(collective_id=0, has_side_effects=True),
        )(queries, keys.reshape(count, TILE, width), values.reshape(count, TILE, width), neighbours, live_tiles, boundary_ids)

    rows = P(("group", "slab"), None)
    return jax.shard_map(
        shards,
        mesh=mesh,
        in_specs=(rows, rows, rows, rows, P(("group", "slab")), rows),
        out_specs=rows,
        check_vma=False,
    )
```
